128 devices in a mesh: mem: 32 (over y, z_hi, x), ty: 2 (over core), tx: 2 (over z_lo).
Axes of the slice: x: 4, y: 4, z: 4 (z_hi: 2, z_lo: 2; z = z_hi * 2 + z_lo), core: 2. Of those that a mesh axis runs over, the one named last changes fastest.
Arguments:
- predicted_states: float32 [512, 3, 64, 512], P('mem', None, 'ty', 'tx'), may hold values from -6 to 6
- undisturbed_thickness_ratio: float32 [64, 512], P('ty', 'tx'), may hold values from 0.5 to 1.5
- sampled_location: int32 [2, 2, 65536], P('ty', 'tx'), may hold values from 0 to 8191
- measured_height: float32 [2, 2, 65536], P('ty', 'tx', 'mem'), may hold values from -6 to 6
- gauge_uncertainty: float32 [2, 2, 65536], P('ty', 'tx', 'mem'), may hold values from 0.5 to 1.5
- gauge_tally: int32 [2, 2, 32], P('ty', 'tx', 'mem'), may hold values from 128 to 2048, as said below
Outputs:
- analysis: bfloat16 [512, 3, 64, 512], P('mem', None, 'ty', 'tx')
The draws below stay inside these ranges and needn't reach their ends.
Inputs may be any that keep to these rules, and one draw needn't show every extreme that they name: `gauge_tally`: every entry is a multiple of 128; in every tile some region has exactly 2048 used slots; the used slots of a region come first. `sampled_location`: A flat index tile row * 256 + tile column within the slot's own tile.
All inputs are finite; a program needn't handle non-finite values.
Results may differ from the reference program's by a relative error of at most 0.012.
The reference program's roundings to bfloat16 on the way count: a program that leaves them out, or rounds other values in their place, can miss the bound.
Values may be sent and summed in bfloat16 or wider, within the bound.
No kernel may reach another device: no remote copies, remote signals or barrier semaphores. Data moves between devices by JAX's collectives and lax.ppermute only.
A program may use at most 128 MiB of HBM per device.

```python
import math
import jax
import jax.numpy as jnp
from jax import lax

TRAJECTORY_TOTAL = 512
CY = 32
CX = 256
OBB = 16
OBLK = 128
NSI = 12
STEPS = 2
MESH_NORTHWARD_N = 64
MESH_EASTWARD_N = 512
RROWS = 1
MAXR = 2048
NOBT = 65536
N_MEM = 32
N_TY = 2
N_TX = 2


def draw_gauge_tally(key, part):
    key_blocks = jax.random.fold_in(key, 11)
    key_fullest = jax.random.fold_in(key, 12)
    blocks = jax.random.randint(key_blocks, (N_TY, N_TX, N_MEM), 1, OBB + 1)
    fullest = jax.random.randint(key_fullest, (N_TY, N_TX, 1), 0, N_MEM)
    position = jnp.arange(N_MEM, dtype=jnp.int32)
    blocks = jnp.where(position == fullest, OBB, blocks)
    return (blocks * OBLK).astype(jnp.int32)


def draw_gauge_uncertainty(key, part):
    lowest = math.log(0.5)
    highest = math.log(1.5)
    spot = jax.random.uniform(jax.random.fold_in(key, 21), (N_TY, N_TX, NOBT), jnp.float32)
    errors = jnp.exp(lowest + (highest - lowest) * spot)
    return jnp.clip(errors, 0.5, 1.5).astype(jnp.float32)


def touch_ends(array, own_key, least, high):
    longest = array.shape.index(max(array.shape))
    spots = []
    for shift in (0, 1):
        where = [jax.random.randint(jax.random.fold_in(own_key, axis), (), 0, length) for axis, length in enumerate(array.shape)]
        where[longest] = (where[longest] + shift) % array.shape[longest]
        spots.append(tuple(where))
    return array.at[spots[0]].set(least).at[spots[1]].set(high)


def block_levels(stream_key, dims, cuts, low, high):
    level = 1.0
    for axis_at, parts in cuts:
        draws = jax.random.uniform(jax.random.fold_in(jax.random.fold_in(stream_key, 6), axis_at), (parts,), jnp.float32, low / len(cuts), high / len(cuts))
        level = level * jnp.repeat(jnp.exp(draws), dims[axis_at] // parts).reshape((-1,) + (1,) * (len(dims) - 1 - axis_at))
    return level


def centred(key, extent, width, limit, pieces=(), kind=jnp.bfloat16):
    values = width * jax.random.normal(key, extent, jnp.float32)
    if pieces:
        values = values * block_levels(key, extent, pieces, -0.22, 0.18)
    return jnp.clip(values, -limit, limit).astype(kind)


def setup_inputs(seed: int = 0) -> dict:
    key_list = jax.random.split(jax.random.key(seed), 7)
    predicted_states = centred(key_list[0], (TRAJECTORY_TOTAL, 3, MESH_NORTHWARD_N, MESH_EASTWARD_N), 1.0, 6.0, ((0, 32), (2, 2), (3, 2)), jnp.float32)
    undisturbed_thickness_ratio = jnp.clip(0.5 + 1.0 * jax.random.uniform(key_list[1], (MESH_NORTHWARD_N, MESH_EASTWARD_N), jnp.float32) ** block_levels(key_list[1], (MESH_NORTHWARD_N, MESH_EASTWARD_N), ((0, 2), (1, 2)), -0.2, 0.2), 0.5, 1.5)
    sampled_location = touch_ends(jax.random.randint(key_list[2], (N_TY, N_TX, NOBT), 0, CY * CX), jax.random.fold_in(key_list[2], 1), 0, (CY * CX) - 1).astype(jnp.int32)
    measured_height = centred(key_list[3], (N_TY, N_TX, NOBT), 1.0, 6.0, ((0, 2), (1, 2), (2, 32)), jnp.float32)
    gauge_uncertainty = draw_gauge_uncertainty(jax.random.fold_in(key_list[6], 71), 0)
    gauge_tally = draw_gauge_tally(jax.random.fold_in(key_list[6], 71), 0)
    return {"predicted_states": predicted_states, "undisturbed_thickness_ratio": undisturbed_thickness_ratio, "sampled_location": sampled_location, "measured_height": measured_height, "gauge_uncertainty": gauge_uncertainty, "gauge_tally": gauge_tally}


HALF_NU = 0.35
ONE_THIRD = 1.0 / 3.0
TWO_THIRD = 2.0 / 3.0

def tendency(padded, depth_inner):
    height = padded[..., 0, :, :]
    zonal = padded[..., 1, :, :]
    meridional = padded[..., 2, :, :]
    divergence = zonal[..., 1:-1, 2:] - zonal[..., 1:-1, :-2] + (meridional[..., 2:, 1:-1] - meridional[..., :-2, 1:-1])
    height_rate = -HALF_NU * depth_inner * divergence
    zonal_rate = -HALF_NU * (height[..., 1:-1, 2:] - height[..., 1:-1, :-2])
    merid_rate = -HALF_NU * (height[..., 2:, 1:-1] - height[..., :-2, 1:-1])
    return jnp.stack([height_rate, zonal_rate, merid_rate], axis=-3)

def starts(*values):
    return tuple((jnp.asarray(value).astype(jnp.int32) for value in values))

def transform_weights(gathered, values, errors, total):
    members = gathered.shape[0]
    slots = gathered.shape[1]
    row_index = jnp.arange(slots, dtype=jnp.int32)
    row_mask = (row_index < total).astype(jnp.float32)
    obs_wide = gathered.astype(jnp.float32)
    obs_mean = lax.optimization_barrier(jnp.mean(obs_wide, axis=0))
    weight_scale = row_mask / errors
    scaled_dev = ((obs_wide - obs_mean) * weight_scale).astype(jnp.bfloat16)
    scaled_innov = ((values - obs_mean) * weight_scale).astype(jnp.bfloat16)
    gram_matrix = jnp.dot(scaled_dev, scaled_dev.T, preferred_element_type=jnp.float32)
    identity_k = jnp.eye(members, dtype=jnp.float32)
    system = gram_matrix + (members - 1.0) * identity_k
    frob_norm = jnp.sqrt(jnp.sum(system * system))
    root_iter = (system / frob_norm).astype(jnp.bfloat16)
    inverse_root = identity_k.astype(jnp.bfloat16)
    for iteration in range(NSI):
        product = jnp.dot(inverse_root, root_iter, preferred_element_type=jnp.float32)
        correction = (1.5 * identity_k - 0.5 * product).astype(jnp.bfloat16)
        root_iter = jnp.dot(root_iter, correction, preferred_element_type=jnp.float32).astype(jnp.bfloat16)
        inverse_root = jnp.dot(correction, inverse_root, preferred_element_type=jnp.float32).astype(jnp.bfloat16)
    projected = jnp.dot(scaled_dev, scaled_innov, preferred_element_type=jnp.float32)
    inverse_wide = inverse_root.astype(jnp.float32)
    inner_step = jnp.dot(inverse_wide, projected, precision=lax.Precision.HIGHEST)
    mean_weights = jnp.dot(inverse_wide, inner_step, precision=lax.Precision.HIGHEST) / frob_norm
    weights = (jnp.sqrt((members - 1.0) / frob_norm) * inverse_wide + mean_weights[:, None]).astype(jnp.bfloat16)
    return weights

def apply_weights(weights, regrouped):
    members = regrouped.shape[0]
    flat = regrouped.reshape(members, -1)
    mean_field = lax.optimization_barrier(jnp.mean(flat.astype(jnp.float32), axis=0))
    deviation = (flat.astype(jnp.float32) - mean_field).astype(jnp.bfloat16)
    mixed = jnp.dot(weights.T, deviation, preferred_element_type=jnp.float32)
    return (mean_field + mixed).astype(jnp.bfloat16).reshape(regrouped.shape)

def reference(predicted_states, undisturbed_thickness_ratio, sampled_location, measured_height, gauge_uncertainty, gauge_tally):

    def wrap_pad(trajectory_states):
        return jnp.pad(trajectory_states, ((0, 0), (1, 1), (1, 1)), mode='wrap')

    def trajectory_prediction(trajectory_states):
        for iteration in range(STEPS):
            first = trajectory_states + tendency(wrap_pad(trajectory_states), undisturbed_thickness_ratio)
            second = 0.75 * trajectory_states + 0.25 * (first + tendency(wrap_pad(first), undisturbed_thickness_ratio))
            trajectory_states = ONE_THIRD * trajectory_states + TWO_THIRD * (second + tendency(wrap_pad(second), undisturbed_thickness_ratio))
        return trajectory_states.astype(jnp.bfloat16)
    background_trajectories = lax.map(trajectory_prediction, predicted_states)

    def region(region_id):
        tile_row = region_id // (N_TX * N_MEM)
        tile_col = region_id // N_MEM % N_TX
        strip = region_id % N_MEM
        tile_height = lax.dynamic_slice(background_trajectories, starts(0, 0, tile_row * CY, tile_col * CX), (TRAJECTORY_TOTAL, 1, CY, CX)).reshape(TRAJECTORY_TOTAL, CY * CX)
        cell_index = lax.dynamic_slice(sampled_location, starts(tile_row, tile_col, strip * MAXR), (1, 1, MAXR)).reshape(MAXR)
        values = lax.dynamic_slice(measured_height, starts(tile_row, tile_col, strip * MAXR), (1, 1, MAXR)).reshape(MAXR)
        errors = lax.dynamic_slice(gauge_uncertainty, starts(tile_row, tile_col, strip * MAXR), (1, 1, MAXR)).reshape(MAXR)
        total = lax.dynamic_slice(gauge_tally, starts(tile_row, tile_col, strip), (1, 1, 1)).reshape(())
        gathered = jnp.take(tile_height, cell_index, axis=1)
        weights = transform_weights(gathered, values, errors, total)
        regrouped = lax.dynamic_slice(background_trajectories, starts(0, 0, tile_row * CY + strip * RROWS, tile_col * CX), (TRAJECTORY_TOTAL, 3, RROWS, CX))
        return apply_weights(weights, regrouped)
    region_ids = jnp.arange(N_TY * N_TX * N_MEM, dtype=jnp.int32)
    results = lax.map(region, region_ids)
    results = results.reshape(N_TY, N_TX, N_MEM, TRAJECTORY_TOTAL, 3, RROWS, CX)
    results = jnp.transpose(results, (3, 4, 0, 2, 5, 1, 6))
    return results.reshape(TRAJECTORY_TOTAL, 3, MESH_NORTHWARD_N, MESH_EASTWARD_N)
```

```python
import jax
import jax.numpy as jnp
from jax import lax
from jax.experimental import pallas as pl
from jax.experimental.pallas import tpu as pltpu
from jax.sharding import PartitionSpec as P

NSI = 12
STEPS = 2
MEMBERS = 512
GROUP = 32
LOCAL = 16
CY = 32
CX = 256
SLOTS = 2048
FIELDS = 3
HALO = 6
WIDE_ROWS = CY + 2 * HALO
WIDE_COLS = CX + 128
PACK = 16
CHUNK = 512

HALF_NU = 0.35
ONE_THIRD = 1.0 / 3.0
TWO_THIRD = 2.0 / 3.0

VMEM_LIMIT = 56 << 20


def edge_lanes(block):
    lane = lax.broadcasted_iota(jnp.int32, block.shape[:-1] + (128,), block.ndim - 1)
    return jnp.where(lane < 64, block[..., :128], block[..., 128:])


def pack_edges(edges, per):
    rows = edges.shape[0]
    total = None
    for place in range(rows // per):
        part = pltpu.roll(edges[place * per : (place + 1) * per], HALO + PACK * place, 2)
        if total is None:
            total = part
        else:
            lane = lax.broadcasted_iota(jnp.int32, part.shape, 2)
            total = jnp.where(lane >= PACK * place, part, total)
    return total


def outgoing_kernel(x_ref, depth_ref, state_ref, rows_ref, cols_ref, corner_ref):
    for field in range(FIELDS):
        state_ref[field] = pltpu.einshape("mrc->rmc", x_ref[:, field])
    depth = depth_ref[...]
    outer = (slice(0, HALO), slice(CY - HALO, CY))
    for field in range(FIELDS):
        block = state_ref[field]
        edges = edge_lanes(block)
        cols_ref[4 * field : 4 * field + 4] = pack_edges(edges, 4)
        both = jnp.concatenate([edges[part] for part in outer], axis=0)
        corner_ref[2 * field : 2 * field + 2] = pack_edges(both, 2)
        rows_ref[12 * field : 12 * field + 6] = block[outer[0]]
        rows_ref[12 * field + 6 : 12 * field + 12] = block[outer[1]]
    depth_edges = edge_lanes(depth)
    cols_ref[12] = depth_edges[:16]
    cols_ref[13] = depth_edges[16:]
    rows_ref[36, 0:HALO] = depth[outer[0]]
    rows_ref[36, HALO : 2 * HALO] = depth[outer[1]]
    rows_ref[36, 2 * HALO : 16] = depth[0:4]
    corner_ref[6, 0:HALO] = depth_edges[outer[0]]
    corner_ref[6, HALO : 2 * HALO] = depth_edges[outer[1]]
    corner_ref[6, 2 * HALO : 16] = depth_edges[0:4]


def forecast_kernel(
    state_ref, depth_ref, rows_ref, cols_ref, corner_ref, cells_ref, strips_ref, base_ref, one_ref, two_ref, rate_ref
):
    upper = slice(0, HALO)
    inner = slice(HALO, HALO + CY)
    lower = slice(HALO + CY, WIDE_ROWS)
    main = slice(0, CX)
    rim = slice(CX, WIDE_COLS)

    for field in range(FIELDS):
        base_ref[field, inner, :, main] = state_ref[field]
        base_ref[field, lower, :, main] = rows_ref[12 * field : 12 * field + 6]
        base_ref[field, upper, :, main] = rows_ref[12 * field + 6 : 12 * field + 12]
        packed = cols_ref[4 * field : 4 * field + 4]
        for place in range(8):
            base_ref[field, HALO + 4 * place : HALO + 4 * place + 4, :, rim] = pltpu.roll(
                packed, 128 - HALO - PACK * place, 2
            )
        packed = corner_ref[2 * field : 2 * field + 2]
        for place in range(6):
            start = HALO + CY + 2 * place if place < 3 else 2 * place - HALO
            base_ref[field, start : start + 2, :, rim] = pltpu.roll(packed, (128 - HALO - PACK * place) % 128, 2)
    rate_ref[inner, main] = -HALF_NU * depth_ref[...]
    rate_ref[lower, main] = -HALF_NU * rows_ref[36, 0:HALO]
    rate_ref[upper, main] = -HALF_NU * rows_ref[36, HALO : 2 * HALO]
    rate_ref[HALO : HALO + 16, rim] = -HALF_NU * cols_ref[12]
    rate_ref[HALO + 16 : HALO + 32, rim] = -HALF_NU * cols_ref[13]
    rate_ref[lower, rim] = -HALF_NU * corner_ref[6, 0:HALO]
    rate_ref[upper, rim] = -HALF_NU * corner_ref[6, HALO : 2 * HALO]

    def shift_zonal(row, carry):
        base_ref[1, row] = pltpu.roll(base_ref[1, row], 1, 1)
        return carry

    lax.fori_loop(0, WIDE_ROWS, shift_zonal, 0, unroll=4)

    def advanced(source, row):
        height = source[0, row]
        zonal = source[1, row]
        divergence = (pltpu.roll(zonal, WIDE_COLS - 2, 1) - zonal) + (source[2, row + 1] - source[2, row - 1])
        height_next = height + rate_ref[pl.ds(row, 1), :] * divergence
        zonal_next = zonal + -HALF_NU * (height - pltpu.roll(height, 2, 1))
        merid_next = source[2, row] + -HALF_NU * (source[0, row + 1] - source[0, row - 1])
        return height_next, zonal_next, merid_next

    def sweep(source, target, old_part, new_part, margin):
        def step(row, carry):
            for field, value in enumerate(advanced(source, row)):
                if old_part is not None:
                    value = old_part * base_ref[field, row] + new_part * value
                target[field, row] = value
            return carry

        lax.fori_loop(margin, WIDE_ROWS - margin, step, 0, unroll=2)

    for iteration in range(STEPS):
        margin = 3 * iteration
        sweep(base_ref, one_ref, None, None, margin + 1)
        sweep(one_ref, two_ref, 0.75, 0.25, margin + 2)
        if iteration + 1 < STEPS:
            sweep(two_ref, base_ref, ONE_THIRD, TWO_THIRD, margin + 3)

    def finish(pair, carry):
        for half in range(2):
            row = 2 * pair + half
            wide = row + HALO
            height, zonal, merid = (
                ONE_THIRD * base_ref[field, wide] + TWO_THIRD * value
                for field, value in enumerate(advanced(two_ref, wide))
            )
            zonal = pltpu.roll(zonal, WIDE_COLS - 1, 1)
            height = height[:, main].astype(jnp.bfloat16)
            cells_ref[pair, :, half * CX : (half + 1) * CX] = height
            strips_ref[row, :, 0:CX] = height
            strips_ref[row, :, CX : 2 * CX] = zonal[:, main].astype(jnp.bfloat16)
            strips_ref[row, :, 2 * CX : 3 * CX] = merid[:, main].astype(jnp.bfloat16)
        return carry

    lax.fori_loop(0, CY // 2, finish, 0)


def sample_kernel(cells_ref, place_ref, out_ref):
    cells = cells_ref[...].reshape(16 * LOCAL, 2 * CX)
    for part in range(SLOTS // CHUNK):
        span = slice(part * CHUNK, (part + 1) * CHUNK)
        place = place_ref[:, span]
        within = place & (2 * CX - 1)
        pair = place >> 9
        pick = (lax.broadcasted_iota(jnp.int32, (2 * CX, CHUNK), 0) == within).astype(jnp.bfloat16)
        product = jnp.dot(cells, pick, preferred_element_type=jnp.float32)
        taken = product[:LOCAL]
        for number in range(1, 16):
            taken = jnp.where(pair == number, product[number * LOCAL : (number + 1) * LOCAL], taken)
        out_ref[0, :, span] = taken.astype(jnp.bfloat16)


def dot32(left, right, dims=((1,), (0,))):
    return lax.dot_general(left, right, (dims, ((), ())), preferred_element_type=jnp.float32)


def exact_product(matrix, column):
    high = column.astype(jnp.bfloat16)
    rest = column - high.astype(jnp.float32)
    middle = rest.astype(jnp.bfloat16)
    low = (rest - middle.astype(jnp.float32)).astype(jnp.bfloat16)
    lane = lax.broadcasted_iota(jnp.int32, (MEMBERS, 128), 1)
    wide = lambda part: jnp.broadcast_to(part.astype(jnp.float32), (MEMBERS, 128))
    parts = jnp.where(lane == 0, wide(high), jnp.where(lane == 1, wide(middle), jnp.where(lane == 2, wide(low), 0.0)))
    return jnp.sum(dot32(matrix, parts.astype(jnp.bfloat16)), axis=1, keepdims=True)


def weights_kernel(total_ref, obs_ref, values_ref, errors_ref, out_ref, dev_ref, root_ref, inverse_ref, correction_ref):
    total = total_ref[0, 0]
    projected = jnp.zeros((MEMBERS, 8), jnp.float32)
    for part in range(SLOTS // CHUNK):
        span = slice(part * CHUNK, (part + 1) * CHUNK)
        obs = obs_ref[:, span].astype(jnp.float32)
        mean = jnp.sum(obs, axis=0, keepdims=True) * (1.0 / MEMBERS)
        slot = lax.broadcasted_iota(jnp.int32, (1, CHUNK), 1) + part * CHUNK
        scale = (slot < total).astype(jnp.float32) / errors_ref[:, span]
        scaled = ((obs - mean) * scale).astype(jnp.bfloat16)
        innovation = ((values_ref[:, span] - mean) * scale).astype(jnp.bfloat16)
        dev_ref[:, span] = scaled
        rows = jnp.broadcast_to(innovation.astype(jnp.float32), (8, CHUNK)).astype(jnp.bfloat16)
        projected = projected + dot32(scaled, rows, ((1,), (1,)))
    diagonal = lax.broadcasted_iota(jnp.int32, (MEMBERS, MEMBERS), 0) == lax.broadcasted_iota(
        jnp.int32, (MEMBERS, MEMBERS), 1
    )
    system = dot32(dev_ref[...], dev_ref[...], ((1,), (1,))) + jnp.where(diagonal, MEMBERS - 1.0, 0.0)
    frob = jnp.sqrt(jnp.sum(system * system, keepdims=True))
    root = (system / frob).astype(jnp.bfloat16)
    root_ref[...] = root

    def corrected(product):
        return (jnp.where(diagonal, 1.5, 0.0) - 0.5 * product).astype(jnp.bfloat16)

    correction = corrected(root.astype(jnp.float32))
    inverse_ref[...] = correction
    root_ref[...] = dot32(root_ref[...], correction).astype(jnp.bfloat16)

    def iterate(index, carry):
        correction_ref[...] = corrected(dot32(inverse_ref[...], root_ref[...]))
        root_ref[...] = dot32(root_ref[...], correction_ref[...]).astype(jnp.bfloat16)
        inverse_ref[...] = dot32(correction_ref[...], inverse_ref[...]).astype(jnp.bfloat16)
        return carry

    lax.fori_loop(0, NSI - 2, iterate, 0)
    correction_ref[...] = corrected(dot32(inverse_ref[...], root_ref[...]))
    inverse = dot32(correction_ref[...], inverse_ref[...]).astype(jnp.bfloat16)
    inner = exact_product(inverse, projected[:, 0:1])
    mean_weights = exact_product(inverse, inner) / frob
    out_ref[...] = (jnp.sqrt((MEMBERS - 1.0) / frob) * inverse.astype(jnp.float32) + mean_weights).astype(jnp.bfloat16)


def update_kernel(weights_ref, strips_ref, out_ref):
    strips = strips_ref[...].astype(jnp.float32)
    mean = jnp.sum(strips, axis=0, keepdims=True) * (1.0 / MEMBERS)
    deviation = (strips - mean).astype(jnp.bfloat16)
    mixed = dot32(weights_ref[...], deviation, ((0,), (0,)))
    out_ref[...] = (mean + mixed).astype(jnp.bfloat16)


VMEM = pl.BlockSpec(memory_space=pltpu.VMEM)
SMEM = pl.BlockSpec(memory_space=pltpu.SMEM)


def shape(dims, kind):
    return jax.ShapeDtypeStruct(dims, kind)


def params():
    return pltpu.CompilerParams(vmem_limit_bytes=VMEM_LIMIT)


def shards(
    predicted_states,
    undisturbed_thickness_ratio,
    sampled_location,
    measured_height,
    gauge_uncertainty,
    gauge_tally,
):
    f32, bf16 = jnp.float32, jnp.bfloat16
    state, rows, cols, corner = pl.pallas_call(
        outgoing_kernel,
        out_shape=(
            shape((FIELDS, CY, LOCAL, CX), f32),
            shape((37, LOCAL, CX), f32),
            shape((14, LOCAL, 128), f32),
            shape((7, LOCAL, 128), f32),
        ),
        in_specs=[VMEM, VMEM],
        out_specs=(VMEM, VMEM, VMEM, VMEM),
        compiler_params=params(),
        name="outgoing",
    )(predicted_states, undisturbed_thickness_ratio)
    rows = lax.ppermute(rows, "ty", [(0, 1), (1, 0)])
    cols = lax.ppermute(cols, "tx", [(0, 1), (1, 0)])
    corner = lax.ppermute(corner, ("ty", "tx"), [(0, 3), (1, 2), (2, 1), (3, 0)])
    wide = (FIELDS, WIDE_ROWS, LOCAL, WIDE_COLS)
    cells, strips = pl.pallas_call(
        forecast_kernel,
        out_shape=(shape((CY // 2, LOCAL, 2 * CX), bf16), shape((CY, LOCAL, FIELDS * CX), bf16)),
        in_specs=[VMEM] * 5,
        out_specs=(VMEM, VMEM),
        scratch_shapes=[pltpu.VMEM(wide, f32)] * 3 + [pltpu.VMEM((WIDE_ROWS + 4, WIDE_COLS), f32)],
        compiler_params=params(),
        name="forecast",
    )(state, undisturbed_thickness_ratio, rows, cols, corner)
    taken = pl.pallas_call(
        sample_kernel,
        grid=(GROUP,),
        out_shape=shape((GROUP, LOCAL, SLOTS), bf16),
        in_specs=[
            pl.BlockSpec((CY // 2, LOCAL, 2 * CX), lambda region: (0, 0, 0)),
            pl.BlockSpec((1, SLOTS), lambda region: (0, region)),
        ],
        out_specs=pl.BlockSpec((1, LOCAL, SLOTS), lambda region: (region, 0, 0)),
        compiler_params=params(),
        name="sample",
    )(cells, sampled_location.reshape(1, GROUP * SLOTS))
    gathered = lax.all_to_all(taken, "mem", 0, 0, tiled=True).reshape(MEMBERS, SLOTS)
    weights = pl.pallas_call(
        weights_kernel,
        out_shape=shape((MEMBERS, MEMBERS), bf16),
        in_specs=[SMEM, VMEM, VMEM, VMEM],
        out_specs=VMEM,
        scratch_shapes=[pltpu.VMEM((MEMBERS, SLOTS), bf16)] + [pltpu.VMEM((MEMBERS, MEMBERS), bf16)] * 3,
        compiler_params=params(),
        name="weights",
    )(
        gauge_tally.reshape(1, 1),
        gathered,
        measured_height.reshape(1, SLOTS),
        gauge_uncertainty.reshape(1, SLOTS),
    )
    regrouped = lax.all_to_all(strips, "mem", 0, 0, tiled=True).reshape(MEMBERS, FIELDS * CX)
    updated = pl.pallas_call(
        update_kernel,
        out_shape=shape((MEMBERS, FIELDS * CX), bf16),
        in_specs=[VMEM, VMEM],
        out_specs=VMEM,
        compiler_params=params(),
        name="update",
    )(weights, regrouped)
    back = lax.all_to_all(updated.reshape(GROUP, LOCAL, FIELDS * CX), "mem", 0, 0, tiled=True)
    return back.reshape(CY, LOCAL, FIELDS, CX).transpose(1, 2, 0, 3)


def solution(mesh):
    in_specs = (
        P("mem", None, "ty", "tx"),
        P("ty", "tx"),
        P("ty", "tx", None),
        P("ty", "tx", "mem"),
        P("ty", "tx", "mem"),
        P("ty", "tx", "mem"),
    )
    out_specs = P("mem", None, "ty", "tx")
    return jax.shard_map(shards, mesh=mesh, in_specs=in_specs, out_specs=out_specs, check_vma=False)
```

```python
import jax
import jax.numpy as jnp
from jax import lax
from jax.experimental import pallas as pl
from jax.experimental.pallas import tpu as pltpu
from jax.sharding import PartitionSpec as P

NSI = 12
STEPS = 2
MEMBERS = 512
GROUP = 32
LOCAL = 16
CY = 32
CX = 256
SLOTS = 2048
FIELDS = 3
BUNDLE = SLOTS + FIELDS * CX
HALO = 6
WIDE_ROWS = CY + 2 * HALO
WIDE_COLS = CX + 128
PACK = 16
CHUNK = 512
PRODUCT = 1536
BY_LANES = (2, 1, 1)

HALF_NU = 0.35
ONE_THIRD = 1.0 / 3.0
TWO_THIRD = 2.0 / 3.0


def edge_lanes(block):
    lane = lax.broadcasted_iota(jnp.int32, block.shape[:-1] + (128,), block.ndim - 1)
    return jnp.where(lane < 64, block[..., :128], block[..., 128:])


def pack_edges(edges, per):
    rows = edges.shape[0]
    total = None
    for place in range(rows // per):
        part = pltpu.roll(edges[place * per : (place + 1) * per], HALO + PACK * place, 2)
        if total is None:
            total = part
        else:
            lane = lax.broadcasted_iota(jnp.int32, part.shape, 2)
            total = jnp.where(lane >= PACK * place, part, total)
    return total


def outgoing_kernel(x_ref, depth_in_ref, state_ref, depth_ref, rows_ref, cols_ref, corner_ref):
    depth = depth_in_ref[...]
    depth_ref[...] = depth
    outer = (slice(0, HALO), slice(CY - HALO, CY))
    for field in range(FIELDS):
        state_ref[field] = pltpu.einshape("mrc->rmc", x_ref[:, field])
        block = state_ref[field]
        edges = edge_lanes(block)
        cols_ref[4 * field : 4 * field + 4] = pack_edges(edges, 4)
        both = jnp.concatenate([edges[part] for part in outer], axis=0)
        corner_ref[2 * field : 2 * field + 2] = pack_edges(both, 2)
        rows_ref[12 * field : 12 * field + 6] = block[outer[0]]
        rows_ref[12 * field + 6 : 12 * field + 12] = block[outer[1]]
    depth_edges = edge_lanes(depth)
    cols_ref[12] = depth_edges[:16]
    cols_ref[13] = depth_edges[16:]
    rows_ref[36, 0:HALO] = depth[outer[0]]
    rows_ref[36, HALO : 2 * HALO] = depth[outer[1]]
    rows_ref[36, 2 * HALO : 16] = depth[0:4]
    corner_ref[6, 0:HALO] = depth_edges[outer[0]]
    corner_ref[6, HALO : 2 * HALO] = depth_edges[outer[1]]
    corner_ref[6, 2 * HALO : 16] = depth_edges[0:4]


def forecast_kernel(
    state_ref, depth_ref, rows_ref, cols_ref, corner_ref, cells_ref, strips_ref, base_ref, one_ref, two_ref, rate_ref
):
    upper = slice(0, HALO)
    inner = slice(HALO, HALO + CY)
    lower = slice(HALO + CY, WIDE_ROWS)
    main = slice(0, CX)
    rim = slice(CX, WIDE_COLS)

    for field in range(FIELDS):
        base_ref[field, inner, :, main] = state_ref[field]
        base_ref[field, lower, :, main] = rows_ref[12 * field : 12 * field + 6]
        base_ref[field, upper, :, main] = rows_ref[12 * field + 6 : 12 * field + 12]
        packed = cols_ref[4 * field : 4 * field + 4]
        for place in range(8):
            base_ref[field, HALO + 4 * place : HALO + 4 * place + 4, :, rim] = pltpu.roll(
                packed, 128 - HALO - PACK * place, 2
            )
        packed = corner_ref[2 * field : 2 * field + 2]
        for place in range(6):
            start = HALO + CY + 2 * place if place < 3 else 2 * place - HALO
            base_ref[field, start : start + 2, :, rim] = pltpu.roll(packed, (128 - HALO - PACK * place) % 128, 2)
    rate_ref[inner, main] = -HALF_NU * depth_ref[...]
    rate_ref[lower, main] = -HALF_NU * rows_ref[36, 0:HALO]
    rate_ref[upper, main] = -HALF_NU * rows_ref[36, HALO : 2 * HALO]
    rate_ref[HALO : HALO + 16, rim] = -HALF_NU * cols_ref[12]
    rate_ref[HALO + 16 : HALO + 32, rim] = -HALF_NU * cols_ref[13]
    rate_ref[lower, rim] = -HALF_NU * corner_ref[6, 0:HALO]
    rate_ref[upper, rim] = -HALF_NU * corner_ref[6, HALO : 2 * HALO]

    def shift_zonal(row, carry):
        base_ref[1, row] = pltpu.roll(base_ref[1, row], 1, 1)
        return carry

    lax.fori_loop(0, WIDE_ROWS, shift_zonal, 0, unroll=11)

    def advanced(source, row):
        height = source[0, row]
        zonal = source[1, row]
        divergence = (pltpu.roll(zonal, WIDE_COLS - 2, 1) - zonal) + (source[2, row + 1] - source[2, row - 1])
        height_next = height + rate_ref[pl.ds(row, 1), :] * divergence
        zonal_next = zonal + -HALF_NU * (height - pltpu.roll(height, 2, 1))
        merid_next = source[2, row] + -HALF_NU * (source[0, row + 1] - source[0, row - 1])
        return height_next, zonal_next, merid_next

    def sweep(source, target, old_part, new_part, margin):
        def step(row, carry):
            for field, value in enumerate(advanced(source, row)):
                if old_part is not None:
                    value = old_part * base_ref[field, row] + new_part * value
                target[field, row] = value
            return carry

        lax.fori_loop(margin, WIDE_ROWS - margin, step, 0, unroll=8)

    for iteration in range(STEPS):
        margin = 3 * iteration
        sweep(base_ref, one_ref, None, None, margin + 1)
        sweep(one_ref, two_ref, 0.75, 0.25, margin + 2)
        if iteration + 1 < STEPS:
            sweep(two_ref, base_ref, ONE_THIRD, TWO_THIRD, margin + 3)

    def finish(pair, carry):
        for half in range(2):
            row = 2 * pair + half
            wide = row + HALO
            height, zonal, merid = (
                ONE_THIRD * base_ref[field, wide] + TWO_THIRD * value
                for field, value in enumerate(advanced(two_ref, wide))
            )
            zonal = pltpu.roll(zonal, WIDE_COLS - 1, 1)
            height = height[:, main].astype(jnp.bfloat16)
            cells_ref[pair, :, half * CX : (half + 1) * CX] = height
            strips_ref[row, :, 0:CX] = height
            strips_ref[row, :, CX : 2 * CX] = zonal[:, main].astype(jnp.bfloat16)
            strips_ref[row, :, 2 * CX : 3 * CX] = merid[:, main].astype(jnp.bfloat16)
        return carry

    lax.fori_loop(0, CY // 2, finish, 0, unroll=4)


def sample_kernel(cells_ref, strips_ref, place_ref, out_ref, halves_ref):
    out_ref[0, :, SLOTS:] = strips_ref[0]

    @pl.when(pl.program_id(0) == 0)
    def _():
        def widen(pair, carry):
            for quarter in range(4):
                halves_ref[4 * pair + quarter] = cells_ref[pair, :, quarter * 128 : (quarter + 1) * 128].astype(jnp.float32)
            return carry

        lax.fori_loop(0, 16, widen, 0)

    cells = cells_ref[...].reshape(16 * LOCAL, 2 * CX)

    def by_product(start, width):
        span = slice(start, start + width)
        place = place_ref[:, span]
        within = place & (2 * CX - 1)
        pair = place >> 9
        hit = lax.broadcasted_iota(jnp.int16, (2 * CX, width), 0) == within.astype(jnp.int16)
        pick = jnp.where(hit, jnp.ones(hit.shape, jnp.bfloat16), jnp.zeros(hit.shape, jnp.bfloat16))
        product = jnp.dot(cells, pick, preferred_element_type=jnp.float32)
        taken = product[:LOCAL]
        for number in range(1, 16):
            taken = jnp.where(pair == number, product[number * LOCAL : (number + 1) * LOCAL], taken)
        out_ref[0, :, span] = taken.astype(jnp.bfloat16)

    def by_lanes(start):
        span = slice(start, start + 128)
        place = place_ref[:, span]
        lane = jnp.broadcast_to(place & 127, (8, 128))
        block = jnp.broadcast_to(place >> 7, (8, 128))
        taken = [jnp.zeros((8, 128), jnp.float32)] * 2
        for number in range(64):
            match = block == number
            for half in range(2):
                source = halves_ref[number, 8 * half : 8 * half + 8, :]
                moved = jnp.take_along_axis(source, lane, axis=1, mode="promise_in_bounds")
                taken[half] = jnp.where(match, moved, taken[half])
        out_ref[0, :, span] = jnp.concatenate(taken, axis=0).astype(jnp.bfloat16)

    for part in range(PRODUCT // CHUNK):
        by_product(part * CHUNK, CHUNK)
        for piece in range(BY_LANES[part]):
            by_lanes(PRODUCT + 128 * (sum(BY_LANES[:part]) + piece))


def dot32(left, right, dims=((1,), (0,))):
    return lax.dot_general(left, right, (dims, ((), ())), preferred_element_type=jnp.float32)


def exact_product(matrix, column):
    high = column.astype(jnp.bfloat16)
    rest = column - high.astype(jnp.float32)
    middle = rest.astype(jnp.bfloat16)
    low = (rest - middle.astype(jnp.float32)).astype(jnp.bfloat16)
    lane = lax.broadcasted_iota(jnp.int32, (MEMBERS, 128), 1)
    wide = lambda part: jnp.broadcast_to(part.astype(jnp.float32), (MEMBERS, 128))
    parts = jnp.where(lane == 0, wide(high), jnp.where(lane == 1, wide(middle), jnp.where(lane == 2, wide(low), 0.0)))
    return jnp.sum(dot32(matrix, parts.astype(jnp.bfloat16)), axis=1, keepdims=True)


def analysis_kernel(
    total_ref, gathered_ref, values_ref, errors_ref, out_ref, dev_ref, root_ref, inverse_ref, correction_ref
):
    total = total_ref[0, 0]
    projected = jnp.zeros((MEMBERS, 8), jnp.float32)
    for part in range(SLOTS // CHUNK):
        span = slice(part * CHUNK, (part + 1) * CHUNK)
        obs = gathered_ref[:, span].astype(jnp.float32)
        mean = jnp.sum(obs, axis=0, keepdims=True) * (1.0 / MEMBERS)
        slot = lax.broadcasted_iota(jnp.int32, (1, CHUNK), 1) + part * CHUNK
        scale = (slot < total).astype(jnp.float32) / errors_ref[:, span]
        scaled = ((obs - mean) * scale).astype(jnp.bfloat16)
        innovation = ((values_ref[:, span] - mean) * scale).astype(jnp.bfloat16)
        dev_ref[:, span] = scaled
        rows = jnp.broadcast_to(innovation.astype(jnp.float32), (8, CHUNK)).astype(jnp.bfloat16)
        projected = projected + dot32(scaled, rows, ((1,), (1,)))
    diagonal = lax.broadcasted_iota(jnp.int32, (MEMBERS, MEMBERS), 0) == lax.broadcasted_iota(
        jnp.int32, (MEMBERS, MEMBERS), 1
    )
    system = dot32(dev_ref[...], dev_ref[...], ((1,), (1,))) + jnp.where(diagonal, MEMBERS - 1.0, 0.0)
    frob = jnp.sqrt(jnp.sum(system * system, keepdims=True))
    root = (system / frob).astype(jnp.bfloat16)
    root_ref[...] = root

    def corrected(product):
        return (jnp.where(diagonal, 1.5, 0.0) - 0.5 * product).astype(jnp.bfloat16)

    correction = corrected(root.astype(jnp.float32))
    inverse_ref[...] = correction
    root_ref[...] = dot32(root_ref[...], correction).astype(jnp.bfloat16)

    def iterate(index, carry):
        correction_ref[...] = corrected(dot32(inverse_ref[...], root_ref[...]))
        root_ref[...] = dot32(root_ref[...], correction_ref[...]).astype(jnp.bfloat16)
        inverse_ref[...] = dot32(correction_ref[...], inverse_ref[...]).astype(jnp.bfloat16)
        return carry

    lax.fori_loop(0, NSI - 2, iterate, 0)
    correction_ref[...] = corrected(dot32(inverse_ref[...], root_ref[...]))
    inverse = dot32(correction_ref[...], inverse_ref[...]).astype(jnp.bfloat16)
    inner = exact_product(inverse, projected[:, 0:1])
    mean_weights = exact_product(inverse, inner) / frob
    root_ref[...] = (jnp.sqrt((MEMBERS - 1.0) / frob) * inverse.astype(jnp.float32) + mean_weights).astype(jnp.bfloat16)
    for part in range(FIELDS):
        span = slice(part * CX, (part + 1) * CX)
        strips = gathered_ref[:, SLOTS + part * CX : SLOTS + (part + 1) * CX].astype(jnp.float32)
        field_mean = jnp.sum(strips, axis=0, keepdims=True) * (1.0 / MEMBERS)
        deviation = (strips - field_mean).astype(jnp.bfloat16)
        mixed = dot32(root_ref[...], deviation, ((0,), (0,)))
        out_ref[:, span] = (field_mean + mixed).astype(jnp.bfloat16)


def deliver_kernel(back_ref, out_ref):
    for field in range(FIELDS):
        out_ref[:, field] = pltpu.einshape("rmc->mrc", back_ref[:, :, field * CX : (field + 1) * CX])


VMEM = pl.BlockSpec(memory_space=pltpu.VMEM)
SMEM = pl.BlockSpec(memory_space=pltpu.SMEM)


def shape(dims, kind):
    return jax.ShapeDtypeStruct(dims, kind)


def params(mebibytes):
    return pltpu.CompilerParams(vmem_limit_bytes=mebibytes << 20)


def shards(
    predicted_states,
    undisturbed_thickness_ratio,
    sampled_location,
    measured_height,
    gauge_uncertainty,
    gauge_tally,
):
    f32, bf16 = jnp.float32, jnp.bfloat16
    state, depth, rows, cols, corner = pl.pallas_call(
        outgoing_kernel,
        out_shape=(
            shape((FIELDS, CY, LOCAL, CX), f32),
            shape((CY, CX), f32),
            shape((37, LOCAL, CX), f32),
            shape((14, LOCAL, 128), f32),
            shape((7, LOCAL, 128), f32),
        ),
        in_specs=[VMEM, VMEM],
        out_specs=(VMEM,) * 5,
        compiler_params=params(12),
        name="outgoing",
    )(predicted_states, undisturbed_thickness_ratio)
    rows = lax.ppermute(rows, "ty", [(0, 1), (1, 0)])
    cols = lax.ppermute(cols, "tx", [(0, 1), (1, 0)])
    corner = lax.ppermute(corner, ("ty", "tx"), [(0, 3), (1, 2), (2, 1), (3, 0)])
    wide = (FIELDS, WIDE_ROWS, LOCAL, WIDE_COLS)
    cells, strips = pl.pallas_call(
        forecast_kernel,
        out_shape=(shape((CY // 2, LOCAL, 2 * CX), bf16), shape((CY, LOCAL, FIELDS * CX), bf16)),
        in_specs=[VMEM] * 5,
        out_specs=(VMEM, VMEM),
        scratch_shapes=[pltpu.VMEM(wide, f32)] * 3 + [pltpu.VMEM((WIDE_ROWS + 4, WIDE_COLS), f32)],
        compiler_params=params(20),
        name="forecast",
    )(state, depth, rows, cols, corner)
    taken = pl.pallas_call(
        sample_kernel,
        grid=(GROUP,),
        out_shape=shape((GROUP, LOCAL, BUNDLE), bf16),
        in_specs=[
            pl.BlockSpec((CY // 2, LOCAL, 2 * CX), lambda region: (0, 0, 0)),
            pl.BlockSpec((1, LOCAL, FIELDS * CX), lambda region: (region, 0, 0)),
            pl.BlockSpec((1, SLOTS), lambda region: (0, region)),
        ],
        out_specs=pl.BlockSpec((1, LOCAL, BUNDLE), lambda region: (region, 0, 0)),
        scratch_shapes=[pltpu.VMEM((64, LOCAL, 128), jnp.float32)],
        compiler_params=params(52),
        name="sample",
    )(cells, strips, sampled_location.reshape(1, GROUP * SLOTS))
    gathered = lax.all_to_all(taken, "mem", 0, 0, tiled=True).reshape(MEMBERS, BUNDLE)
    updated = pl.pallas_call(
        analysis_kernel,
        out_shape=shape((MEMBERS, FIELDS * CX), bf16),
        in_specs=[SMEM, VMEM, VMEM, VMEM],
        out_specs=VMEM,
        scratch_shapes=[pltpu.VMEM((MEMBERS, SLOTS), bf16)] + [pltpu.VMEM((MEMBERS, MEMBERS), bf16)] * 3,
        compiler_params=params(24),
        name="analysis",
    )(
        gauge_tally.reshape(1, 1),
        gathered,
        measured_height.reshape(1, SLOTS),
        gauge_uncertainty.reshape(1, SLOTS),
    )
    back = lax.all_to_all(updated.reshape(GROUP, LOCAL, FIELDS * CX), "mem", 0, 0, tiled=True)
    return pl.pallas_call(
        deliver_kernel,
        out_shape=shape((LOCAL, FIELDS, CY, CX), bf16),
        in_specs=[VMEM],
        out_specs=VMEM,
        compiler_params=params(8),
        name="deliver",
    )(back)


def solution(mesh):
    in_specs = (
        P("mem", None, "ty", "tx"),
        P("ty", "tx"),
        P("ty", "tx", None),
        P("ty", "tx", "mem"),
        P("ty", "tx", "mem"),
        P("ty", "tx", "mem"),
    )
    out_specs = P("mem", None, "ty", "tx")
    return jax.shard_map(shards, mesh=mesh, in_specs=in_specs, out_specs=out_specs, check_vma=False)
```

```python
import jax
import jax.numpy as jnp
from jax import lax
from jax.experimental import pallas as pl
from jax.experimental.pallas import tpu as pltpu
from jax.sharding import PartitionSpec as P


NSI = 12
STEPS = 2
MEMBERS = 512
GROUP = 32
LOCAL = 16
CY = 32
CX = 256
SLOTS = 2048
FIELDS = 3
BUNDLE = SLOTS + FIELDS * CX
HALO = 6
WIDE_ROWS = CY + 2 * HALO
WIDE_COLS = CX + 128
EDGE = 2 * HALO
COL_SLABS = 10
CORNER_SLABS = 4
CHUNK = 512
PRODUCT = 1536
BY_LANES = (2, 1, 1)

HALF_NU = 0.35
ONE_THIRD = 1.0 / 3.0
TWO_THIRD = 2.0 / 3.0


def edge_lanes(block):
    lane = lax.broadcasted_iota(jnp.int32, block.shape[:-1] + (128,), block.ndim - 1)
    return jnp.where(lane < 64, block[..., :128], block[..., 128:])


def pack_edges(edges, per):
    count = edges.shape[0]
    total = pltpu.roll(edges[:per], HALO, 2)
    for place in range(1, pl.cdiv(count, per)):
        part = edges[place * per : min((place + 1) * per, count)]
        size = part.shape[0]
        lane = lax.broadcasted_iota(jnp.int32, part.shape, 2)
        mixed = jnp.where(lane >= EDGE * place, pltpu.roll(part, HALO + EDGE * place, 2), total[:size])
        total = mixed if size == per else jnp.concatenate([mixed, total[size:]], axis=0)
    return total


def runs(count, per, size):
    for place in range(pl.cdiv(count, per)):
        at = place * per
        end = min(at + per, count)
        while at < end:
            field, row = divmod(at, size)
            length = min(end - at, size - row)
            yield place, at - place * per, field, row, length
            at += length


def outgoing_kernel(x_ref, rate_ref, state_ref, rows_ref, cols_ref, corner_ref):
    rate = rate_ref[...]
    state_ref[FIELDS * CY] = rate[:16]
    state_ref[FIELDS * CY + 1] = rate[16:]
    outer = (slice(0, HALO), slice(CY - HALO, CY))
    edges, corners = [], []
    for field in range(FIELDS):
        block = pltpu.einshape("mrc->rmc", x_ref[:, field])
        state_ref[field * CY : (field + 1) * CY] = block
        edges.append(edge_lanes(block))
        corners.extend(edges[field][part] for part in outer)
        rows_ref[12 * field : 12 * field + 6] = block[outer[0]]
        rows_ref[12 * field + 6 : 12 * field + 12] = block[outer[1]]
    cols_ref[:COL_SLABS] = pack_edges(jnp.concatenate(edges, axis=0), COL_SLABS)
    corner_ref[:CORNER_SLABS] = pack_edges(jnp.concatenate(corners, axis=0), CORNER_SLABS)
    rate_edges = edge_lanes(rate)
    lane = lax.broadcasted_iota(jnp.int32, (LOCAL, 128), 1)
    cols_ref[COL_SLABS] = jnp.where(
        lane < EDGE, pltpu.roll(rate_edges[:16], HALO, 1), pltpu.roll(rate_edges[16:], HALO + EDGE, 1)
    )
    rows_ref[36, 0:HALO] = rate[outer[0]]
    rows_ref[36, HALO : 2 * HALO] = rate[outer[1]]
    rows_ref[36, 2 * HALO : 16] = rate[0:4]
    corner_ref[CORNER_SLABS, 0:HALO] = rate_edges[outer[0]]
    corner_ref[CORNER_SLABS, HALO : 2 * HALO] = rate_edges[outer[1]]
    corner_ref[CORNER_SLABS, 2 * HALO : 16] = rate_edges[0:4]


def forecast_kernel(
    state_ref, rows_ref, cols_ref, corner_ref, cells_ref, strips_ref, base_ref, one_ref, two_ref, rate_ref
):
    upper = slice(0, HALO)
    inner = slice(HALO, HALO + CY)
    lower = slice(HALO + CY, WIDE_ROWS)
    main = slice(0, CX)
    rim = slice(CX, WIDE_COLS)

    for field in range(FIELDS):
        base_ref[field, inner, :, main] = state_ref[field * CY : (field + 1) * CY]
        base_ref[field, lower, :, main] = rows_ref[12 * field : 12 * field + 6]
        base_ref[field, upper, :, main] = rows_ref[12 * field + 6 : 12 * field + 12]
    for place, slab, field, row, length in runs(FIELDS * CY, COL_SLABS, CY):
        base_ref[field, HALO + row : HALO + row + length, :, rim] = pltpu.roll(
            cols_ref[slab : slab + length], 128 - HALO - EDGE * place, 2
        )
    for place, slab, field, row, length in runs(FIELDS * 2 * HALO, CORNER_SLABS, 2 * HALO):
        moved = pltpu.roll(corner_ref[slab : slab + length], 128 - HALO - EDGE * place, 2)
        for step in range(length):
            start = HALO + CY + row + step if row + step < HALO else row + step - HALO
            base_ref[field, start, :, rim] = moved[step]
    rate_ref[HALO : HALO + 16, main] = state_ref[FIELDS * CY]
    rate_ref[HALO + 16 : HALO + 32, main] = state_ref[FIELDS * CY + 1]
    rate_ref[lower, main] = rows_ref[36, 0:HALO]
    rate_ref[upper, main] = rows_ref[36, HALO : 2 * HALO]
    packed = cols_ref[COL_SLABS]
    rate_ref[HALO : HALO + 16, rim] = pltpu.roll(packed, 128 - HALO, 1)
    rate_ref[HALO + 16 : HALO + 32, rim] = pltpu.roll(packed, 128 - HALO - EDGE, 1)
    rate_ref[lower, rim] = corner_ref[CORNER_SLABS, 0:HALO]
    rate_ref[upper, rim] = corner_ref[CORNER_SLABS, HALO : 2 * HALO]

    def shift_zonal(row, carry):
        base_ref[1, row] = pltpu.roll(base_ref[1, row], 1, 1)
        return carry

    lax.fori_loop(0, WIDE_ROWS, shift_zonal, 0, unroll=11)

    def advanced(source, row):
        height = source[0, row]
        zonal = source[1, row]
        divergence = (pltpu.roll(zonal, WIDE_COLS - 2, 1) - zonal) + (source[2, row + 1] - source[2, row - 1])
        height_next = height + rate_ref[pl.ds(row, 1), :] * divergence
        zonal_next = zonal + -HALF_NU * (height - pltpu.roll(height, 2, 1))
        merid_next = source[2, row] + -HALF_NU * (source[0, row + 1] - source[0, row - 1])
        return height_next, zonal_next, merid_next

    def sweep(source, target, old_part, new_part, margin):
        def step(row, carry):
            for field, value in enumerate(advanced(source, row)):
                if old_part is not None:
                    value = old_part * base_ref[field, row] + new_part * value
                target[field, row] = value
            return carry

        lax.fori_loop(margin, WIDE_ROWS - margin, step, 0, unroll=8)

    for iteration in range(STEPS):
        margin = 3 * iteration
        sweep(base_ref, one_ref, None, None, margin + 1)
        sweep(one_ref, two_ref, 0.75, 0.25, margin + 2)
        if iteration + 1 < STEPS:
            sweep(two_ref, base_ref, ONE_THIRD, TWO_THIRD, margin + 3)

    def finish(pair, carry):
        for half in range(2):
            row = 2 * pair + half
            wide = row + HALO
            height, zonal, merid = (
                ONE_THIRD * base_ref[field, wide] + TWO_THIRD * value
                for field, value in enumerate(advanced(two_ref, wide))
            )
            zonal = pltpu.roll(zonal, WIDE_COLS - 1, 1)
            height = height[:, main].astype(jnp.bfloat16)
            cells_ref[pair, :, half * CX : (half + 1) * CX] = height
            strips_ref[row, :, 0:CX] = height
            strips_ref[row, :, CX : 2 * CX] = zonal[:, main].astype(jnp.bfloat16)
            strips_ref[row, :, 2 * CX : 3 * CX] = merid[:, main].astype(jnp.bfloat16)
        return carry

    lax.fori_loop(0, CY // 2, finish, 0, unroll=4)


def sample_kernel(cells_ref, strips_ref, place_ref, out_ref, halves_ref):
    out_ref[0, :, SLOTS:] = strips_ref[0]

    @pl.when(pl.program_id(0) == 0)
    def _():
        def widen(pair, carry):
            for quarter in range(4):
                halves_ref[4 * pair + quarter] = cells_ref[pair, :, quarter * 128 : (quarter + 1) * 128].astype(jnp.float32)
            return carry

        lax.fori_loop(0, 16, widen, 0)

    cells = cells_ref[...].reshape(16 * LOCAL, 2 * CX)

    def by_product(start, width):
        span = slice(start, start + width)
        place = place_ref[:, span]
        within = place & (2 * CX - 1)
        pair = place >> 9
        hit = lax.broadcasted_iota(jnp.int16, (2 * CX, width), 0) == within.astype(jnp.int16)
        pick = jnp.where(hit, jnp.ones(hit.shape, jnp.bfloat16), jnp.zeros(hit.shape, jnp.bfloat16))
        product = jnp.dot(cells, pick, preferred_element_type=jnp.float32)
        taken = product[:LOCAL]
        for number in range(1, 16):
            taken = jnp.where(pair == number, product[number * LOCAL : (number + 1) * LOCAL], taken)
        out_ref[0, :, span] = taken.astype(jnp.bfloat16)

    def by_lanes(start):
        span = slice(start, start + 128)
        place = place_ref[:, span]
        lane = jnp.broadcast_to(place & 127, (8, 128))
        block = jnp.broadcast_to(place >> 7, (8, 128))
        taken = [jnp.zeros((8, 128), jnp.float32)] * 2
        for number in range(64):
            match = block == number
            for half in range(2):
                source = halves_ref[number, 8 * half : 8 * half + 8, :]
                moved = jnp.take_along_axis(source, lane, axis=1, mode="promise_in_bounds")
                taken[half] = jnp.where(match, moved, taken[half])
        out_ref[0, :, span] = jnp.concatenate(taken, axis=0).astype(jnp.bfloat16)

    for part in range(PRODUCT // CHUNK):
        by_product(part * CHUNK, CHUNK)
        for piece in range(BY_LANES[part]):
            by_lanes(PRODUCT + 128 * (sum(BY_LANES[:part]) + piece))


def dot32(left, right, dims=((1,), (0,))):
    return lax.dot_general(left, right, (dims, ((), ())), preferred_element_type=jnp.float32)


def exact_product(row, matrix):
    high = row.astype(jnp.bfloat16).astype(jnp.float32)
    middle = (row - high).astype(jnp.bfloat16).astype(jnp.float32)
    low = row - high - middle
    line = lax.broadcasted_iota(jnp.int32, (LOCAL, MEMBERS), 0)
    parts = jnp.where(line == 0, high, jnp.where(line == 1, middle, jnp.where(line == 2, low, 0.0)))
    return jnp.sum(dot32(parts.astype(jnp.bfloat16), matrix), axis=0, keepdims=True)


def analysis_kernel(
    total_ref, gathered_ref, values_ref, errors_ref, out_ref, dev_ref, root_ref, inverse_ref, correction_ref
):
    prior = slice(0, SLOTS)

    def add_rows(block, partial):
        rows = gathered_ref[pl.ds(block * LOCAL, LOCAL), prior].astype(jnp.float32)
        return partial + (rows[:8] + rows[8:])

    blocks = MEMBERS // LOCAL
    partial = lax.fori_loop(0, blocks, add_rows, jnp.zeros((8, SLOTS), jnp.float32), unroll=2)
    mean = jnp.sum(partial, axis=0, keepdims=True) * (1.0 / MEMBERS)
    slot = lax.broadcasted_iota(jnp.int32, (1, SLOTS), 1)
    scale = (slot < total_ref[0, 0]).astype(jnp.float32) / errors_ref[...]
    innovation = (values_ref[...] - mean) * scale
    dev_ref[MEMBERS:, :] = jnp.broadcast_to(innovation, (LOCAL, SLOTS)).astype(jnp.bfloat16)

    def center_rows(block, carry):
        span = pl.ds(block * LOCAL, LOCAL)
        rows = gathered_ref[span, prior].astype(jnp.float32)
        dev_ref[span, :] = ((rows - mean) * scale).astype(jnp.bfloat16)
        return carry

    lax.fori_loop(0, blocks, center_rows, 0, unroll=2)
    products = dot32(dev_ref[...], dev_ref[:MEMBERS, :], ((1,), (1,)))
    projected = products[MEMBERS : MEMBERS + 1]
    diagonal = lax.broadcasted_iota(jnp.int32, (MEMBERS, MEMBERS), 0) == lax.broadcasted_iota(
        jnp.int32, (MEMBERS, MEMBERS), 1
    )
    system = products[:MEMBERS] + jnp.where(diagonal, MEMBERS - 1.0, 0.0)
    frob = jnp.sqrt(jnp.sum(system * system, keepdims=True))
    root = (system / frob).astype(jnp.bfloat16)
    root_ref[...] = root

    def corrected(product):
        return (jnp.where(diagonal, 1.5, 0.0) - 0.5 * product).astype(jnp.bfloat16)

    correction = corrected(root.astype(jnp.float32))
    inverse_ref[...] = correction
    root_ref[...] = dot32(root_ref[...], correction).astype(jnp.bfloat16)

    def iterate(index, carry):
        correction = corrected(dot32(inverse_ref[...], root_ref[...]))
        correction_ref[...] = correction
        new_inverse = dot32(correction_ref[...], inverse_ref[...]).astype(jnp.bfloat16)
        root_ref[...] = dot32(root_ref[...], correction).astype(jnp.bfloat16)
        inverse_ref[...] = new_inverse
        return carry

    lax.fori_loop(0, NSI - 2, iterate, 0, unroll=10)
    correction_ref[...] = corrected(dot32(inverse_ref[...], root_ref[...]))
    root_ref[...] = dot32(correction_ref[...], inverse_ref[...]).astype(jnp.bfloat16).T
    inner = exact_product(projected, root_ref[...])
    mean_weights = exact_product(inner, root_ref[...]) / frob
    inverse_ref[...] = (
        jnp.sqrt((MEMBERS - 1.0) / frob) * root_ref[...].astype(jnp.float32) + mean_weights
    ).astype(jnp.bfloat16)
    for part in range(FIELDS):
        span = slice(part * CX, (part + 1) * CX)
        strips = gathered_ref[:, SLOTS + part * CX : SLOTS + (part + 1) * CX].astype(jnp.float32)
        field_mean = jnp.sum(strips, axis=0, keepdims=True) * (1.0 / MEMBERS)
        deviation = (strips - field_mean).astype(jnp.bfloat16)
        mixed = dot32(inverse_ref[...], deviation)
        out_ref[:, span] = (field_mean + mixed).astype(jnp.bfloat16)


def deliver_kernel(back_ref, out_ref):
    for field in range(FIELDS):
        out_ref[:, field] = pltpu.einshape("rmc->mrc", back_ref[:, :, field * CX : (field + 1) * CX])


VMEM = pl.BlockSpec(memory_space=pltpu.VMEM)
SMEM = pl.BlockSpec(memory_space=pltpu.SMEM)


def shape(dims, kind):
    return jax.ShapeDtypeStruct(dims, kind)


def params(mebibytes):
    return pltpu.CompilerParams(vmem_limit_bytes=mebibytes << 20)


def hop(value, pairs, axis):
    return lax.ppermute(value, axis, pairs)


def shards(
    predicted_states,
    undisturbed_thickness_ratio,
    sampled_location,
    measured_height,
    gauge_uncertainty,
    gauge_tally,
):
    f32, bf16 = jnp.float32, jnp.bfloat16
    state, rows, cols, corner = pl.pallas_call(
        outgoing_kernel,
        out_shape=(
            shape((FIELDS * CY + 2, LOCAL, CX), f32),
            shape((37, LOCAL, CX), f32),
            shape((COL_SLABS + 1, LOCAL, 128), f32),
            shape((CORNER_SLABS + 1, LOCAL, 128), f32),
        ),
        in_specs=[VMEM, VMEM],
        out_specs=(VMEM,) * 4,
        compiler_params=params(12),
        name="outgoing",
    )(predicted_states, -HALF_NU * undisturbed_thickness_ratio)
    cols = hop(cols, [(0, 1), (1, 0)], "tx")
    corner = hop(corner, [(0, 3), (1, 2), (2, 1), (3, 0)], ("ty", "tx"))
    rows = hop(rows, [(0, 1), (1, 0)], "ty")
    wide = (FIELDS, WIDE_ROWS, LOCAL, WIDE_COLS)
    cells, strips = pl.pallas_call(
        forecast_kernel,
        out_shape=(shape((CY // 2, LOCAL, 2 * CX), bf16), shape((CY, LOCAL, FIELDS * CX), bf16)),
        in_specs=[VMEM] * 4,
        out_specs=(VMEM, VMEM),
        scratch_shapes=[pltpu.VMEM(wide, f32)] * 3 + [pltpu.VMEM((WIDE_ROWS + 4, WIDE_COLS), f32)],
        compiler_params=params(20),
        name="forecast",
    )(state, rows, cols, corner)
    taken = pl.pallas_call(
        sample_kernel,
        grid=(GROUP,),
        out_shape=shape((GROUP, LOCAL, BUNDLE), bf16),
        in_specs=[
            pl.BlockSpec((CY // 2, LOCAL, 2 * CX), lambda region: (0, 0, 0)),
            pl.BlockSpec((1, LOCAL, FIELDS * CX), lambda region: (region, 0, 0)),
            pl.BlockSpec((1, SLOTS), lambda region: (0, region)),
        ],
        out_specs=pl.BlockSpec((1, LOCAL, BUNDLE), lambda region: (region, 0, 0)),
        scratch_shapes=[pltpu.VMEM((64, LOCAL, 128), jnp.float32)],
        compiler_params=params(52),
        name="sample",
    )(cells, strips, sampled_location.reshape(1, GROUP * SLOTS))
    gathered = lax.all_to_all(taken, "mem", 0, 0, tiled=True).reshape(MEMBERS, BUNDLE)
    updated = pl.pallas_call(
        analysis_kernel,
        out_shape=shape((MEMBERS, FIELDS * CX), bf16),
        in_specs=[SMEM, VMEM, VMEM, VMEM],
        out_specs=VMEM,
        scratch_shapes=[pltpu.VMEM((MEMBERS + LOCAL, SLOTS), bf16)] + [pltpu.VMEM((MEMBERS, MEMBERS), bf16)] * 3,
        compiler_params=params(24),
        name="analysis",
    )(
        gauge_tally.reshape(1, 1),
        gathered,
        measured_height.reshape(1, SLOTS),
        gauge_uncertainty.reshape(1, SLOTS),
    )
    back = lax.all_to_all(updated.reshape(GROUP, LOCAL, FIELDS * CX), "mem", 0, 0, tiled=True)
    return pl.pallas_call(
        deliver_kernel,
        out_shape=shape((LOCAL, FIELDS, CY, CX), bf16),
        in_specs=[VMEM],
        out_specs=VMEM,
        compiler_params=params(8),
        name="deliver",
    )(back)


def solution(mesh):
    in_specs = (
        P("mem", None, "ty", "tx"),
        P("ty", "tx"),
        P("ty", "tx", None),
        P("ty", "tx", "mem"),
        P("ty", "tx", "mem"),
        P("ty", "tx", "mem"),
    )
    out_specs = P("mem", None, "ty", "tx")
    return jax.shard_map(shards, mesh=mesh, in_specs=in_specs, out_specs=out_specs, check_vma=False)
```

```python
import jax
import jax.numpy as jnp
from jax import lax
from jax.experimental import pallas as pl
from jax.experimental.pallas import tpu as pltpu
from jax.sharding import PartitionSpec as P


NSI = 12
STEPS = 2
MEMBERS = 512
GROUP = 32
LOCAL = 16
CY = 32
CX = 256
SLOTS = 2048
FIELDS = 3
BUNDLE = SLOTS + FIELDS * CX
HALO = 6
WIDE_ROWS = CY + 2 * HALO
WIDE_COLS = CX + 128
EDGE = 2 * HALO
COL_SLABS = 10
CORNER_SLABS = 4
PRODUCT = 1536
SAMPLE_STEPS = ((512, 2), (512, 1), (512, 1))
REGIONS = 2
PARTS = 2

HALF_NU = 0.35
ONE_THIRD = 1.0 / 3.0
TWO_THIRD = 2.0 / 3.0


def edge_lanes(block):
    lane = lax.broadcasted_iota(jnp.int32, block.shape[:-1] + (128,), block.ndim - 1)
    return jnp.where(lane < 64, block[..., :128], block[..., 128:])


def pack_edges(edges, per):
    count = edges.shape[0]
    total = pltpu.roll(edges[:per], HALO, 2)
    for place in range(1, pl.cdiv(count, per)):
        part = edges[place * per : min((place + 1) * per, count)]
        size = part.shape[0]
        lane = lax.broadcasted_iota(jnp.int32, part.shape, 2)
        mixed = jnp.where(lane >= EDGE * place, pltpu.roll(part, HALO + EDGE * place, 2), total[:size])
        total = mixed if size == per else jnp.concatenate([mixed, total[size:]], axis=0)
    return total


def runs(count, per, size):
    for place in range(pl.cdiv(count, per)):
        at = place * per
        end = min(at + per, count)
        while at < end:
            field, row = divmod(at, size)
            length = min(end - at, size - row)
            yield place, at - place * per, field, row, length
            at += length


def outgoing_kernel(x_ref, rate_ref, state_ref, rows_ref, cols_ref, corner_ref):
    rate = rate_ref[...]
    state_ref[FIELDS * CY] = rate[:16]
    state_ref[FIELDS * CY + 1] = rate[16:]
    outer = (slice(0, HALO), slice(CY - HALO, CY))
    edges, corners = [], []
    for field in range(FIELDS):
        block = pltpu.einshape("mrc->rmc", x_ref[:, field])
        state_ref[field * CY : (field + 1) * CY] = block
        edges.append(edge_lanes(block))
        corners.extend(edges[field][part] for part in outer)
        rows_ref[12 * field : 12 * field + 6] = block[outer[0]]
        rows_ref[12 * field + 6 : 12 * field + 12] = block[outer[1]]
    cols_ref[:COL_SLABS] = pack_edges(jnp.concatenate(edges, axis=0), COL_SLABS)
    corner_ref[:CORNER_SLABS] = pack_edges(jnp.concatenate(corners, axis=0), CORNER_SLABS)
    rate_edges = edge_lanes(rate)
    lane = lax.broadcasted_iota(jnp.int32, (LOCAL, 128), 1)
    cols_ref[COL_SLABS] = jnp.where(
        lane < EDGE, pltpu.roll(rate_edges[:16], HALO, 1), pltpu.roll(rate_edges[16:], HALO + EDGE, 1)
    )
    rows_ref[36, 0:HALO] = rate[outer[0]]
    rows_ref[36, HALO : 2 * HALO] = rate[outer[1]]
    rows_ref[36, 2 * HALO : 16] = rate[0:4]
    corner_ref[CORNER_SLABS, 0:HALO] = rate_edges[outer[0]]
    corner_ref[CORNER_SLABS, HALO : 2 * HALO] = rate_edges[outer[1]]
    corner_ref[CORNER_SLABS, 2 * HALO : 16] = rate_edges[0:4]


def forecast_kernel(
    state_ref, rows_ref, cols_ref, corner_ref, cells_ref, strips_ref, base_ref, one_ref, two_ref, rate_ref
):
    upper = slice(0, HALO)
    inner = slice(HALO, HALO + CY)
    lower = slice(HALO + CY, WIDE_ROWS)
    main = slice(0, CX)
    rim = slice(CX, WIDE_COLS)

    for field in range(FIELDS):
        base_ref[field, inner, :, main] = state_ref[field * CY : (field + 1) * CY]
        base_ref[field, lower, :, main] = rows_ref[12 * field : 12 * field + 6]
        base_ref[field, upper, :, main] = rows_ref[12 * field + 6 : 12 * field + 12]
    for place, slab, field, row, length in runs(FIELDS * CY, COL_SLABS, CY):
        base_ref[field, HALO + row : HALO + row + length, :, rim] = pltpu.roll(
            cols_ref[slab : slab + length], 128 - HALO - EDGE * place, 2
        )
    for place, slab, field, row, length in runs(FIELDS * 2 * HALO, CORNER_SLABS, 2 * HALO):
        moved = pltpu.roll(corner_ref[slab : slab + length], 128 - HALO - EDGE * place, 2)
        for step in range(length):
            start = HALO + CY + row + step if row + step < HALO else row + step - HALO
            base_ref[field, start, :, rim] = moved[step]
    rate_ref[HALO : HALO + 16, main] = state_ref[FIELDS * CY]
    rate_ref[HALO + 16 : HALO + 32, main] = state_ref[FIELDS * CY + 1]
    rate_ref[lower, main] = rows_ref[36, 0:HALO]
    rate_ref[upper, main] = rows_ref[36, HALO : 2 * HALO]
    packed = cols_ref[COL_SLABS]
    rate_ref[HALO : HALO + 16, rim] = pltpu.roll(packed, 128 - HALO, 1)
    rate_ref[HALO + 16 : HALO + 32, rim] = pltpu.roll(packed, 128 - HALO - EDGE, 1)
    rate_ref[lower, rim] = corner_ref[CORNER_SLABS, 0:HALO]
    rate_ref[upper, rim] = corner_ref[CORNER_SLABS, HALO : 2 * HALO]

    def shift_zonal(row, carry):
        base_ref[1, row] = pltpu.roll(base_ref[1, row], 1, 1)
        return carry

    lax.fori_loop(0, WIDE_ROWS, shift_zonal, 0, unroll=11)

    def advanced(source, row):
        height = source[0, row]
        zonal = source[1, row]
        divergence = (pltpu.roll(zonal, WIDE_COLS - 2, 1) - zonal) + (source[2, row + 1] - source[2, row - 1])
        height_next = height + rate_ref[pl.ds(row, 1), :] * divergence
        zonal_next = zonal + -HALF_NU * (height - pltpu.roll(height, 2, 1))
        merid_next = source[2, row] + -HALF_NU * (source[0, row + 1] - source[0, row - 1])
        return height_next, zonal_next, merid_next

    def sweep(source, target, old_part, new_part, margin):
        def step(row, carry):
            for field, value in enumerate(advanced(source, row)):
                if old_part is not None:
                    value = old_part * base_ref[field, row] + new_part * value
                target[field, row] = value
            return carry

        lax.fori_loop(margin, WIDE_ROWS - margin, step, 0, unroll=8)

    for iteration in range(STEPS):
        margin = 3 * iteration
        sweep(base_ref, one_ref, None, None, margin + 1)
        sweep(one_ref, two_ref, 0.75, 0.25, margin + 2)
        if iteration + 1 < STEPS:
            sweep(two_ref, base_ref, ONE_THIRD, TWO_THIRD, margin + 3)

    def finish(pair, carry):
        for half in range(2):
            row = 2 * pair + half
            wide = row + HALO
            height, zonal, merid = (
                ONE_THIRD * base_ref[field, wide] + TWO_THIRD * value
                for field, value in enumerate(advanced(two_ref, wide))
            )
            zonal = pltpu.roll(zonal, WIDE_COLS - 1, 1)
            height = height[:, main].astype(jnp.bfloat16)
            cells_ref[pair, :, half * CX : (half + 1) * CX] = height
            strips_ref[row, :, 0:CX] = height
            strips_ref[row, :, CX : 2 * CX] = zonal[:, main].astype(jnp.bfloat16)
            strips_ref[row, :, 2 * CX : 3 * CX] = merid[:, main].astype(jnp.bfloat16)
        return carry

    lax.fori_loop(0, CY // 2, finish, 0, unroll=4)


def sample_kernel(cells_ref, strips_ref, place_ref, out_ref, halves_ref):
    @pl.when(pl.program_id(0) == 0)
    def _():
        def widen(pair, carry):
            for quarter in range(4):
                halves_ref[4 * pair + quarter] = cells_ref[pair, :, quarter * 128 : (quarter + 1) * 128].astype(jnp.float32)
            return carry

        lax.fori_loop(0, 16, widen, 0)

    out_ref[:, :, SLOTS:] = strips_ref[...]
    cells = cells_ref[...].reshape(16 * LOCAL, 2 * CX)

    def by_product(region, start, width):
        place = place_ref[:, region * SLOTS + start : region * SLOTS + start + width]
        within = place & (2 * CX - 1)
        pair = place >> 9
        hit = lax.broadcasted_iota(jnp.int16, (2 * CX, width), 0) == within.astype(jnp.int16)
        pick = jnp.where(hit, jnp.ones(hit.shape, jnp.bfloat16), jnp.zeros(hit.shape, jnp.bfloat16))
        product = jnp.dot(cells, pick, preferred_element_type=jnp.float32)
        taken = product[:LOCAL]
        for number in range(1, 16):
            taken = jnp.where(pair == number, product[number * LOCAL : (number + 1) * LOCAL], taken)
        out_ref[region, :, start : start + width] = taken.astype(jnp.bfloat16)

    def by_lanes(region, start):
        place = place_ref[:, region * SLOTS + start : region * SLOTS + start + 128]
        lane = jnp.broadcast_to(place & 127, (8, 128))
        block = jnp.broadcast_to(place >> 7, (8, 128))
        taken = [jnp.zeros((8, 128), jnp.float32)] * 2
        for number in range(64):
            match = block == number
            for half in range(2):
                source = halves_ref[number, 8 * half : 8 * half + 8, :]
                moved = jnp.take_along_axis(source, lane, axis=1, mode="promise_in_bounds")
                taken[half] = jnp.where(match, moved, taken[half])
        out_ref[region, :, start : start + 128] = jnp.concatenate(taken, axis=0).astype(jnp.bfloat16)

    for region in range(REGIONS):
        start, rest = 0, PRODUCT
        for width, count in SAMPLE_STEPS:
            by_product(region, start, width)
            start += width
            for _ in range(count):
                by_lanes(region, rest)
                rest += 128


def dot32(left, right, dims=((1,), (0,))):
    return lax.dot_general(left, right, (dims, ((), ())), preferred_element_type=jnp.float32)


def exact_product(row, matrix):
    high = row.astype(jnp.bfloat16).astype(jnp.float32)
    middle = (row - high).astype(jnp.bfloat16).astype(jnp.float32)
    low = row - high - middle
    line = lax.broadcasted_iota(jnp.int32, (LOCAL, MEMBERS), 0)
    parts = jnp.where(line == 0, high, jnp.where(line == 1, middle, jnp.where(line == 2, low, 0.0)))
    return jnp.sum(dot32(parts.astype(jnp.bfloat16), matrix), axis=0, keepdims=True)


def analysis_kernel(
    total_ref, gathered_ref, values_ref, errors_ref, out_ref, dev_ref, root_ref, inverse_ref, correction_ref
):
    slot = lax.broadcasted_iota(jnp.int32, (1, SLOTS), 1)
    every = (slot < total_ref[0, 0]).astype(jnp.float32) / errors_ref[...]
    products = None
    blocks = MEMBERS // LOCAL
    width = SLOTS // PARTS
    for part in range(PARTS):
        span = slice(part * width, (part + 1) * width)
        sums = [jnp.zeros((8, width), jnp.float32) for _ in range(2)]
        for block in range(blocks):
            rows = gathered_ref[block * LOCAL : (block + 1) * LOCAL, span].astype(jnp.float32)
            sums = [sums[0] + rows[:8], sums[1] + rows[8:]]
        mean = jnp.sum(sums[0] + sums[1], axis=0, keepdims=True) * (1.0 / MEMBERS)
        scale = every[:, span]
        innovation = (values_ref[:, span] - mean) * scale
        dev_ref[MEMBERS:, span] = jnp.broadcast_to(innovation, (LOCAL, width)).astype(jnp.bfloat16)
        for block in range(blocks):
            lines = slice(block * LOCAL, (block + 1) * LOCAL)
            rows = gathered_ref[lines, span].astype(jnp.float32)
            dev_ref[lines, span] = ((rows - mean) * scale).astype(jnp.bfloat16)
        product = dot32(dev_ref[:, span], dev_ref[:MEMBERS, span], ((1,), (1,)))
        products = product if products is None else products + product
    projected = products[MEMBERS : MEMBERS + 1]
    diagonal = lax.broadcasted_iota(jnp.int32, (MEMBERS, MEMBERS), 0) == lax.broadcasted_iota(
        jnp.int32, (MEMBERS, MEMBERS), 1
    )
    system = products[:MEMBERS] + jnp.where(diagonal, MEMBERS - 1.0, 0.0)
    frob = jnp.sqrt(jnp.sum(system * system, keepdims=True))
    root = (system / frob).astype(jnp.bfloat16)
    root_ref[...] = root

    def corrected(product):
        return (jnp.where(diagonal, 1.5, 0.0) - 0.5 * product).astype(jnp.bfloat16)

    correction = corrected(root.astype(jnp.float32))
    inverse_ref[...] = correction
    root_ref[...] = dot32(root_ref[...], correction).astype(jnp.bfloat16)

    def iterate(index, carry):
        correction = corrected(dot32(inverse_ref[...], root_ref[...]))
        correction_ref[...] = correction
        new_inverse = dot32(correction_ref[...], inverse_ref[...]).astype(jnp.bfloat16)
        root_ref[...] = dot32(root_ref[...], correction).astype(jnp.bfloat16)
        inverse_ref[...] = new_inverse
        return carry

    lax.fori_loop(0, NSI - 2, iterate, 0, unroll=10)
    correction_ref[...] = corrected(dot32(inverse_ref[...], root_ref[...]))
    root_ref[...] = dot32(correction_ref[...], inverse_ref[...]).astype(jnp.bfloat16).T
    inner = exact_product(projected, root_ref[...])
    mean_weights = exact_product(inner, root_ref[...]) / frob
    inverse_ref[...] = (
        jnp.sqrt((MEMBERS - 1.0) / frob) * root_ref[...].astype(jnp.float32) + mean_weights
    ).astype(jnp.bfloat16)
    for part in range(FIELDS):
        span = slice(part * CX, (part + 1) * CX)
        strips = gathered_ref[:, SLOTS + part * CX : SLOTS + (part + 1) * CX].astype(jnp.float32)
        field_mean = jnp.sum(strips, axis=0, keepdims=True) * (1.0 / MEMBERS)
        deviation = (strips - field_mean).astype(jnp.bfloat16)
        mixed = dot32(inverse_ref[...], deviation)
        out_ref[:, span] = (field_mean + mixed).astype(jnp.bfloat16)


def deliver_kernel(back_ref, out_ref):
    for field in range(FIELDS):
        out_ref[:, field] = pltpu.einshape("rmc->mrc", back_ref[:, :, field * CX : (field + 1) * CX])


VMEM = pl.BlockSpec(memory_space=pltpu.VMEM)
SMEM = pl.BlockSpec(memory_space=pltpu.SMEM)


def shape(dims, kind):
    return jax.ShapeDtypeStruct(dims, kind)


def params(mebibytes):
    return pltpu.CompilerParams(vmem_limit_bytes=mebibytes << 20)


def hop(value, pairs, axis):
    return lax.ppermute(value, axis, pairs)


def shards(
    predicted_states,
    undisturbed_thickness_ratio,
    sampled_location,
    measured_height,
    gauge_uncertainty,
    gauge_tally,
):
    f32, bf16 = jnp.float32, jnp.bfloat16
    state, rows, cols, corner = pl.pallas_call(
        outgoing_kernel,
        out_shape=(
            shape((FIELDS * CY + 2, LOCAL, CX), f32),
            shape((37, LOCAL, CX), f32),
            shape((COL_SLABS + 1, LOCAL, 128), f32),
            shape((CORNER_SLABS + 1, LOCAL, 128), f32),
        ),
        in_specs=[VMEM, VMEM],
        out_specs=(VMEM,) * 4,
        compiler_params=params(12),
        name="outgoing",
    )(predicted_states, -HALF_NU * undisturbed_thickness_ratio)
    cols = hop(cols, [(0, 1), (1, 0)], "tx")
    corner = hop(corner, [(0, 3), (1, 2), (2, 1), (3, 0)], ("ty", "tx"))
    rows = hop(rows, [(0, 1), (1, 0)], "ty")
    wide = (FIELDS, WIDE_ROWS, LOCAL, WIDE_COLS)
    cells, strips = pl.pallas_call(
        forecast_kernel,
        out_shape=(shape((CY // 2, LOCAL, 2 * CX), bf16), shape((CY, LOCAL, FIELDS * CX), bf16)),
        in_specs=[VMEM] * 4,
        out_specs=(VMEM, VMEM),
        scratch_shapes=[pltpu.VMEM(wide, f32)] * 3 + [pltpu.VMEM((WIDE_ROWS + 4, WIDE_COLS), f32)],
        compiler_params=params(20),
        name="forecast",
    )(state, rows, cols, corner)
    taken = pl.pallas_call(
        sample_kernel,
        grid=(GROUP // REGIONS,),
        out_shape=shape((GROUP, LOCAL, BUNDLE), bf16),
        in_specs=[
            pl.BlockSpec((CY // 2, LOCAL, 2 * CX), lambda region: (0, 0, 0)),
            pl.BlockSpec((REGIONS, LOCAL, FIELDS * CX), lambda region: (region, 0, 0)),
            pl.BlockSpec((1, REGIONS * SLOTS), lambda region: (0, region)),
        ],
        out_specs=pl.BlockSpec((REGIONS, LOCAL, BUNDLE), lambda region: (region, 0, 0)),
        scratch_shapes=[pltpu.VMEM((64, LOCAL, 128), jnp.float32)],
        compiler_params=params(52),
        name="sample",
    )(cells, strips, sampled_location.reshape(1, GROUP * SLOTS))
    gathered = lax.all_to_all(taken, "mem", 0, 0, tiled=True).reshape(MEMBERS, BUNDLE)
    updated = pl.pallas_call(
        analysis_kernel,
        out_shape=shape((MEMBERS, FIELDS * CX), bf16),
        in_specs=[SMEM, VMEM, VMEM, VMEM],
        out_specs=VMEM,
        scratch_shapes=[pltpu.VMEM((MEMBERS + LOCAL, SLOTS), bf16)] + [pltpu.VMEM((MEMBERS, MEMBERS), bf16)] * 3,
        compiler_params=params(24),
        name="analysis",
    )(
        gauge_tally.reshape(1, 1),
        gathered,
        measured_height.reshape(1, SLOTS),
        gauge_uncertainty.reshape(1, SLOTS),
    )
    back = lax.all_to_all(updated.reshape(GROUP, LOCAL, FIELDS * CX), "mem", 0, 0, tiled=True)
    return pl.pallas_call(
        deliver_kernel,
        out_shape=shape((LOCAL, FIELDS, CY, CX), bf16),
        in_specs=[VMEM],
        out_specs=VMEM,
        compiler_params=params(8),
        name="deliver",
    )(back)


def solution(mesh):
    in_specs = (
        P("mem", None, "ty", "tx"),
        P("ty", "tx"),
        P("ty", "tx", None),
        P("ty", "tx", "mem"),
        P("ty", "tx", "mem"),
        P("ty", "tx", "mem"),
    )
    out_specs = P("mem", None, "ty", "tx")
    return jax.shard_map(shards, mesh=mesh, in_specs=in_specs, out_specs=out_specs, check_vma=False)
```
